32 devices in a mesh: src: 4 (over y, core), tgt: 8 (over z, x).
Axes of the slice: x: 2, y: 2, z: 4, core: 2. Of those that a mesh axis runs over, the one named last changes fastest.
Arguments:
- src_vel: bfloat16 [2, 48, 131072], P(None, None, ('src', 'tgt')), may hold values from -6 to 6
- angle: float32 [131072], P(('src', 'tgt')), may hold values from -3.140625 to 3.140625
- src_block: int32 [4, 8, 8, 8], P('src', 'tgt'), may hold values from 0 to 31
- tgt_block: int32 [4, 8, 8, 8], P('src', 'tgt'), may hold values from 0 to 31
- send_count: int32 [4, 8, 8], P('src', 'tgt'), may hold values from 0 to 8, as said below
- intersection: bfloat16 [4, 8, 8, 8, 128, 128], P('src', 'tgt'), may hold values from -0.375 to 0.375
- eofs: bfloat16 [512, 2, 131072], P(None, None, ('src', 'tgt')), may hold values from -0.0234375 to 0.0234375
Outputs:
- remapped: bfloat16 [2, 48, 131072], P(None, None, ('src', 'tgt'))
- pcs: float32 [48, 512], P(None, 'tgt')
The draws below stay inside these ranges and needn't reach their ends.
Inputs may be any that keep to these rules, and one draw needn't show every extreme that they name: `src_block`: indices of the sending device's own source blocks. `tgt_block`: indices of the receiving device's target blocks. `send_count`: in every tile row, one receiver column gets 8 live slots from every sender of the row.
All inputs are finite; a program needn't handle non-finite values.
Results may differ from the reference program's by a relative error of at most 0.0058.
Values may be sent and summed in bfloat16 or wider, within the bound.
A program may use at most 64 MiB of HBM per device.

```python
import jax
import jax.numpy as jnp
from jax import lax

BLK = 128
SB = 32
TB = 32
CAP = 8
K = 512
TL = 48
SCELLS = 131072
TCELLS = 131072
N_SRC = 4
N_TGT = 8


def draw_send_count(key, part):
    first_key, second_key = jax.random.split(jax.random.fold_in(key, 11))
    base = jax.random.randint(first_key, (N_SRC, N_TGT, N_TGT), 0, CAP + 1)
    full_col = jax.random.randint(second_key, (N_SRC, 1, 1), 0, N_TGT)
    column = lax.broadcasted_iota(jnp.int32, (N_SRC, N_TGT, N_TGT), 2)
    return jnp.where(column == full_col, CAP, base).astype(jnp.int32)


def set_ends(drawn, own_key, smallest, top_value):
    shape = drawn.shape
    spot = [jax.random.randint(jax.random.fold_in(own_key, axis), (), 0, shape[axis]) for axis in range(len(shape))]
    drawn = drawn.at[tuple(spot)].set(smallest)
    longest = shape.index(max(shape))
    spot[longest] = (spot[longest] + 1) % shape[longest]
    return drawn.at[tuple(spot)].set(top_value)


def with_spikes(values, own_key, source, target, shards_of, factor):
    def block_of(dim):
        return (jnp.arange(values.shape[dim]) // (values.shape[dim] // shards_of)).reshape((-1,) + (1,) * (values.ndim - 1 - dim))

    near = jax.random.permutation(own_key, shards_of)[block_of(target)]
    far = (block_of(target) + shards_of // 2) % shards_of
    return jnp.where((block_of(source) == near) | (block_of(source) == far), factor * values, values)


def level_of(own_key, extent, pieces, least, top_value):
    gain, own = 1.0, jax.random.fold_in(own_key, 6)
    for dim, parts in pieces:
        steps = jnp.exp(jax.random.uniform(jax.random.fold_in(own, dim), (parts,), jnp.float32, least / len(pieces), top_value / len(pieces)))
        gain = gain * jnp.repeat(steps, extent[dim] // parts).reshape([-1 if axis == dim else 1 for axis in range(len(extent))])
    return gain


def normal_values(own_key, extent, scale, bound, cuts=(), kind=jnp.bfloat16):
    array = jax.random.normal(own_key, extent, jnp.float32) * scale
    if len(cuts) > 0:
        array = level_of(own_key, extent, cuts, -0.22, 0.18) * array
    return jnp.clip(array, min=-bound, max=bound).astype(kind)


def heavy_noise(stream_key, shape, spread, reach, cuts, heavy, held_as=jnp.bfloat16):
    values = spread * jax.random.normal(stream_key, shape, jnp.float32)
    if cuts:
        values = values * level_of(stream_key, shape, cuts, -0.22, 0.18)
    return jnp.clip(with_spikes(values, jax.random.fold_in(stream_key, 3), *heavy), -reach, reach).astype(held_as)


def setup_inputs(seed: int = 0) -> dict:
    key_of = jax.random.split(jax.random.key(seed), 8)
    src_vel = normal_values(key_of[0], (2, TL, SCELLS), 1.0, 6.0, ((2, 32),))
    angle = jnp.clip(jax.random.uniform(key_of[1], (SCELLS,), jnp.float32, -3.140625, 3.140625), -3.140625, 3.140625)
    src_block = set_ends(jax.random.randint(key_of[2], (N_SRC, N_TGT, N_TGT, CAP), 0, SB), jax.random.fold_in(key_of[2], 1), 0, SB - 1).astype(jnp.int32)
    tgt_block = set_ends(jax.random.randint(key_of[3], (N_SRC, N_TGT, N_TGT, CAP), 0, TB), jax.random.fold_in(key_of[3], 1), 0, TB - 1).astype(jnp.int32)
    send_count = draw_send_count(jax.random.fold_in(key_of[7], 71), 0)
    intersection = normal_values(key_of[5], (N_SRC, N_TGT, N_TGT, CAP, BLK, BLK), (2 * BLK) ** -0.5, 0.375, ((0, 4), (1, 8)))
    eofs = heavy_noise(key_of[6], (K, 2, TCELLS), (2 * TCELLS) ** -0.5, 0.0234375, ((2, 32),), (2, 0, 32, 2.75))
    return dict(src_vel=src_vel, angle=angle, src_block=src_block, tgt_block=tgt_block, send_count=send_count, intersection=intersection, eofs=eofs)


def remap_row(rotated_row, ids_src, ids_tgt, counts, weights):
    tgt_count = ids_src.shape[0]
    slot_cap = ids_src.shape[2]
    take_index = ids_src.reshape(1, 1, tgt_count, tgt_count * slot_cap, 1).astype(jnp.int32)
    blocks = jnp.take_along_axis(rotated_row, take_index, axis=3)
    weight_rows = weights.reshape(tgt_count, tgt_count * slot_cap, BLK, BLK).astype(jnp.float32)
    contribs = jnp.einsum('ctspi,spij->spctj', blocks.astype(jnp.float32), weight_rows).astype(jnp.bfloat16)
    slot_iota = jnp.arange(slot_cap, dtype=jnp.int32)
    live_slot = slot_iota[None, None, :] < counts[:, :, None]
    target_id = jnp.where(live_slot, ids_tgt, TB)
    onehot = (target_id[..., None] == jnp.arange(TB, dtype=jnp.int32)).astype(jnp.float32)
    contrib_six = contribs.reshape(tgt_count, tgt_count, slot_cap, 2, TL, BLK).astype(jnp.float32)
    return jnp.einsum('sdcb,sdcxyj->xydbj', onehot, contrib_six)


def reference(src_vel, angle, src_block, tgt_block, send_count, intersection, eofs):
    velocity = src_vel.astype(jnp.float32).reshape(2, TL, N_SRC, N_TGT, SB, BLK)
    fold_row = velocity[:, :, N_SRC - 1, :, SB - 1, :]
    mirror = fold_row[:, :, ::-1, ::-1]
    velocity = velocity.at[:, :, N_SRC - 1, :, SB - 1, :].set(0.5 * (fold_row - mirror))
    angles = angle.reshape(N_SRC, N_TGT, SB, BLK)
    cosine = jnp.cos(angles)
    sine_part = jnp.sin(angles)
    zonal = velocity[0]
    meridional = velocity[1]
    eastward = cosine * zonal - sine_part * meridional
    northward = sine_part * zonal + cosine * meridional
    rotated = jnp.stack([eastward, northward]).astype(jnp.bfloat16)
    rot_rows = jnp.moveaxis(rotated, 2, 0)

    def one_row(packed):
        return remap_row(packed[0], packed[1], packed[2], packed[3], packed[4])

    summed = lax.map(one_row, (rot_rows, src_block, tgt_block, send_count, intersection))
    summed = jnp.moveaxis(summed, 0, 2)
    remapped = summed.reshape(2, TL, TCELLS).astype(jnp.bfloat16)
    field_rows = jnp.transpose(remapped, (1, 0, 2)).reshape(TL, 2 * TCELLS)
    eof_rows = eofs.reshape(K, 2 * TCELLS)
    pcs = lax.dot_general(field_rows, eof_rows, (((1,), (1,)), ((), ())), preferred_element_type=jnp.float32)
    return remapped, pcs
```

```python
import functools

import jax
import jax.numpy as jnp
from jax import lax
from jax.experimental import pallas as pl
from jax.experimental.pallas import tpu as pltpu
from jax.sharding import PartitionSpec as P

BLK = 128
PARTS = 2
MESH = pl.DeviceIdType.MESH
NT_DIMS = (((1,), (1,)), ((), ()))


def xor_of(index, mask, count):
    result, bit = 0, 1
    while bit < count:
        result = result + (((index // bit) + (mask // bit)) % 2) * bit
        bit *= 2
    return result


def send_orders(n, nx):
    nz = n // nx
    zs = list(range(1, nz))
    near, far = [z for z in zs if z < nz // 2], [z for z in zs if z >= nz // 2]
    far = far[::-1]

    def masks(steps):
        return [z * nx + x for z in steps for x in range(nx)]

    line = list(range(1, nx))
    inner = masks(far[:1]) + masks(near) + line + masks(far[1:])
    outer = masks(near) + line + masks(far)
    waits = line + masks(near) + masks(far)
    return inner, outer, waits


def kernel(
    n, ns, vel_hbm, angle_hbm, sblk_hbm, tblk_hbm, count_hbm, w_hbm, eofs_hbm,
    out_ref, pcs_ref,
    angle_ref, sblk_ref, tblk_ref, count_ref, vel, w, eo, flat, mirror, cs, sn, rot, send, recv, ids, rids, sids, kron, res, piece, rpiece, rq,
    in_sem, vel_sem, w_sem, eo_sem, fold_sem, tx_sem, rx_sem, idtx_sem, idrx_sem, ids_sem,
    ptx_sem, prx_sem, qtx_sem, qrx_sem,
):
    s, t = lax.axis_index("src"), lax.axis_index("tgt")
    comps, rows, cells = vel.shape
    sb = cells // BLK
    cap = w.shape[1]
    nt, kk2 = flat.shape[0], flat.shape[1]
    tb = nt
    group = BLK // cap
    both = comps * rows
    nx = max(1, ns // 2)
    nz = n // nx
    z = t // nx
    outer = jnp.logical_or(z == 0, z == nz - 1)
    inner_order, outer_order, waits = send_orders(n, nx)
    order = [jnp.where(outer, b, a) for a, b in zip(inner_order, outer_order)] + [0]
    everyone = list(range(1, n))
    peer = {m: xor_of(t, m, n) for m in range(n)}

    vel_copy = pltpu.make_async_copy(vel_hbm, vel, vel_sem)
    vel_copy.start()
    small = [
        pltpu.make_async_copy(angle_hbm, angle_ref, in_sem.at[0]),
        pltpu.make_async_copy(tblk_hbm, tblk_ref, in_sem.at[1]),
        pltpu.make_async_copy(sblk_hbm, sblk_ref, in_sem.at[2]),
        pltpu.make_async_copy(count_hbm, count_ref, in_sem.at[3]),
    ]
    for copy in small:
        copy.start()

    def w_copy(k):
        return pltpu.make_async_copy(w_hbm.at[xor_of(t, order[k], n)], w.at[k], w_sem.at[k])

    for k in range(n):
        w_copy(k).start()

    barrier = pltpu.get_barrier_semaphore()
    for m in everyone:
        pl.semaphore_signal(barrier, inc=1, device_id=(s, peer[m]), device_id_type=MESH)
    for i in range(1, ns):
        pl.semaphore_signal(barrier, inc=1, device_id=((s + i) % ns, t), device_id_type=MESH)

    for copy in small:
        copy.wait()
    cs[...] = jnp.cos(angle_ref[...])
    sn[...] = jnp.sin(angle_ref[...])
    lane_slot = lax.broadcasted_iota(jnp.int32, (8, BLK), 1) // group

    def own_ids(p, carry):
        tile = jnp.zeros((8, BLK), jnp.int32)
        for j in range(cap):
            tile = jnp.where(lane_slot == j, tblk_ref[p, j], tile)
        ids[p] = tile
        return carry

    lax.fori_loop(0, n, own_ids, 0)
    vel_copy.wait()

    def rotate(b, carry):
        lanes = pl.ds(pl.multiple_of(b * BLK, BLK), BLK)
        c, d = cs[pl.ds(b, 1), :], sn[pl.ds(b, 1), :]
        x = vel[0, :, lanes].astype(jnp.float32)
        y = vel[1, :, lanes].astype(jnp.float32)
        rot[b, 0:rows, :] = (c * x - d * y).astype(jnp.bfloat16)
        rot[b, rows:both, :] = (d * x + c * y).astype(jnp.bfloat16)
        return carry

    lax.fori_loop(0, sb, rotate, 0, unroll=2)
    pl.semaphore_wait(barrier, n - 1 + ns - 1)

    def fold_copy():
        return pltpu.make_async_remote_copy(
            src_ref=vel_hbm.at[:, :, pl.ds(cells - BLK, BLK)],
            dst_ref=mirror,
            send_sem=fold_sem.at[0],
            recv_sem=fold_sem.at[1],
            device_id=(s, n - 1 - t),
            device_id_type=MESH,
        )

    @pl.when(s == ns - 1)
    def _():
        fold_copy().start()

    id_copies = {}
    for m in everyone:
        id_copies[m] = pltpu.make_async_remote_copy(
            src_ref=ids.at[peer[m]],
            dst_ref=rids.at[m],
            send_sem=idtx_sem.at[m],
            recv_sem=idrx_sem.at[m],
            device_id=(s, peer[m]),
            device_id_type=MESH,
        )
        id_copies[m].start()

    @pl.when(s == ns - 1)
    def _():
        fold_copy().wait()
        flip = (
            lax.broadcasted_iota(jnp.int32, (BLK, BLK), 0)
            + lax.broadcasted_iota(jnp.int32, (BLK, BLK), 1)
            == BLK - 1
        )
        flip = jnp.where(flip, 1.0, 0.0).astype(jnp.bfloat16)
        parts = []
        for comp in range(comps):
            flipped = jnp.dot(mirror[comp], flip, preferred_element_type=jnp.float32)
            own = vel[comp, :, cells - BLK : cells].astype(jnp.float32)
            parts.append(0.5 * (own - flipped))
        c, d = cs[sb - 1 : sb, :], sn[sb - 1 : sb, :]
        x, y = parts
        rot[sb - 1, 0:rows, :] = (c * x - d * y).astype(jnp.bfloat16)
        rot[sb - 1, rows:both, :] = (d * x + c * y).astype(jnp.bfloat16)

    span = cap // PARTS

    def contribute(k, h, dest, at):
        p = xor_of(t, order[k], n)

        def slot(i, carry):
            j = h * span + i
            block = rot[sblk_ref[p, j]]
            value = jnp.dot(block, w[k, j], preferred_element_type=jnp.float32)
            value = jnp.where(j < count_ref[p], value, 0.0)
            dest[at, j] = value.astype(jnp.bfloat16)
            return carry

        lax.fori_loop(0, span, slot, 0, unroll=True)

    def send_copy(k, m, h):
        part = pl.ds(h * span, span)
        return pltpu.make_async_remote_copy(
            src_ref=send.at[k, part],
            dst_ref=recv.at[m, part],
            send_sem=tx_sem.at[k, h],
            recv_sem=rx_sem.at[m, h],
            device_id=(s, xor_of(t, m, n)),
            device_id_type=MESH,
        )

    for k in range(n - 1):
        w_copy(k).wait()
        for h in range(PARTS):
            contribute(k, h, send, k)
            send_copy(k, order[k], h).start()

    def eo_copy(i):
        return pltpu.make_async_copy(eofs_hbm.at[:, i], eo.at[i], eo_sem.at[i])

    def start_eo(i, carry):
        eo_copy(i).start()
        return carry

    lax.fori_loop(0, nt, start_eo, 0)
    w_copy(n - 1).wait()
    for h in range(PARTS):
        contribute(n - 1, h, recv, 0)

    def stage(i, carry):
        eo_copy(i).wait()
        flat[i] = eo[i].reshape(kk2, BLK)
        return carry

    lax.fori_loop(0, nt, stage, 0)

    diagonal = (
        lax.broadcasted_iota(jnp.int32, (group, BLK), 1) % group
        == lax.broadcasted_iota(jnp.int32, (group, BLK), 0)
    )

    def place(m, tile):
        wide = jnp.concatenate([tile] * (group // 8), axis=0)

        def per_block(b, carry):
            hit = jnp.where((wide == b) & diagonal, 1.0, 0.0).astype(jnp.bfloat16)
            kron[pl.ds(pl.multiple_of(b * group, group), group), m * BLK : (m + 1) * BLK] = hit
            return carry

        lax.fori_loop(0, tb, per_block, 0, unroll=4)

    place(0, ids[t])
    to_scalars = {}
    for m in everyone:
        id_copies[m].wait()
        to_scalars[m] = pltpu.make_async_copy(rids.at[m], sids.at[m], ids_sem.at[m])
        to_scalars[m].start()
        place(m, rids[m])
    for m in everyone:
        to_scalars[m].wait()

    chunk = min(512, kk2)

    def product(m, h, first):
        slots = range(h * span, (h + 1) * span)
        blocks = [tblk_ref[t, j] if m == 0 else sids[m, 0, j * group] for j in slots]
        right = jnp.concatenate([recv[m, j] for j in slots], axis=1)

        def piece_of(i, carry):
            at = pl.ds(pl.multiple_of(i * chunk, chunk), chunk)
            left = jnp.concatenate([flat[b, at, :] for b in blocks], axis=1)
            value = lax.dot_general(left, right, NT_DIMS, preferred_element_type=jnp.float32)
            res[at, 0:both] = value if first else res[at, 0:both] + value
            return carry

        lax.fori_loop(0, kk2 // chunk, piece_of, 0)

    for h in range(PARTS):
        product(0, h, h == 0)
    for m in waits:
        for h in range(PARTS):
            send_copy(0, m, h).wait_recv()
            product(m, h, False)

    kb = kk2 // comps // n
    half = kb // 2
    for d in range(n):
        for h in range(2):
            base = comps * (d * kb + h * half)
            first = res[pl.ds(base, half, stride=2), :]
            second = res[pl.ds(base + 1, half, stride=2), :]
            part = first[:, 0:rows] + second[:, rows:both]
            piece[d, :, h * rows : (h + 1) * rows] = part.astype(piece.dtype)

    ptx = []
    for m in everyone[::-1]:
        copy = pltpu.make_async_remote_copy(
            src_ref=piece.at[peer[m]],
            dst_ref=rpiece.at[m],
            send_sem=ptx_sem.at[m],
            recv_sem=prx_sem.at[m],
            device_id=(s, peer[m]),
            device_id_type=MESH,
        )
        copy.start()
        ptx.append(copy)

    for r in range(0, both, group):
        right = recv[:, :, r : r + group, :].reshape(n * cap * group, BLK)
        summed = jnp.dot(kron[...], right, preferred_element_type=jnp.float32)
        comp, row = r // rows, r % rows
        for b in range(tb):
            out_ref[comp, row : row + group, b * BLK : (b + 1) * BLK] = summed[
                b * group : (b + 1) * group, :
            ].astype(jnp.bfloat16)

    for copy in ptx:
        copy.wait()
    total = piece[t].astype(jnp.float32)
    for m in everyone:
        total = total + rpiece[m].astype(jnp.float32)
    rq[s] = total
    qtx = []
    for i in range(1, ns):
        copy = pltpu.make_async_remote_copy(
            src_ref=rq.at[s],
            dst_ref=rq.at[s],
            send_sem=qtx_sem.at[i],
            recv_sem=qrx_sem.at[i],
            device_id=((s + i) % ns, t),
            device_id_type=MESH,
        )
        copy.start()
        qtx.append(copy)
    for copy in qtx:
        copy.wait()
    final = rq[0]
    for i in range(1, ns):
        final = final + rq[i]
    final = jnp.concatenate([final[:, 0:rows], final[:, rows:both]], axis=0)
    pcs_ref[...] = final.T
    for k in range(n - 1):
        for h in range(PARTS):
            send_copy(k, order[k], h).wait_send()


def per_device(n, ns, src_vel, angle, src_block, tgt_block, send_count, intersection, eofs):
    comps, rows, cells = src_vel.shape
    cap = src_block.shape[3]
    kk, _, tcells = eofs.shape
    tb, nt, sb = tcells // BLK, tcells // BLK, cells // BLK
    eo = eofs.reshape(kk, comps, nt, BLK).transpose(0, 2, 1, 3)
    both = comps * rows
    kb = kk // n
    bf, f32 = jnp.bfloat16, jnp.float32
    vmem, dma = pltpu.VMEM, pltpu.SemaphoreType.DMA
    outside = pl.BlockSpec(memory_space=pltpu.HBM)
    smem = pltpu.SMEM
    inside = pl.BlockSpec(memory_space=pltpu.VMEM)
    remapped, pcs = pl.pallas_call(
        functools.partial(kernel, n, ns),
        out_shape=(
            jax.ShapeDtypeStruct((comps, rows, tcells), bf),
            jax.ShapeDtypeStruct((rows, kb), f32),
        ),
        in_specs=[
            outside, outside, outside, outside, outside, outside, outside,
        ],
        out_specs=(inside, inside),
        scratch_shapes=[
            vmem((sb, BLK), f32),
            smem((n, cap), jnp.int32),
            smem((n, cap), jnp.int32),
            smem((n,), jnp.int32),
            vmem((comps, rows, cells), bf),
            vmem((n, cap, BLK, BLK), bf),
            vmem((nt, kk, comps, BLK), bf),
            vmem((nt, comps * kk, BLK), bf),
            vmem((comps, rows, BLK), bf),
            vmem((sb, BLK), f32),
            vmem((sb, BLK), f32),
            vmem((sb, both, BLK), bf),
            vmem((n - 1, cap, both, BLK), bf),
            vmem((n, cap, both, BLK), bf),
            vmem((n, 8, BLK), jnp.int32),
            vmem((n, 8, BLK), jnp.int32),
            smem((n, 8, BLK), jnp.int32),
            vmem((tb * (BLK // cap), n * BLK), bf),
            vmem((comps * kk, BLK), f32),
            vmem((n, kb // 2, BLK), bf),
            vmem((n, kb // 2, BLK), bf),
            vmem((ns, kb // 2, BLK), f32),
            dma((4,)), dma, dma((n,)), dma((nt,)), dma((2,)), dma((n, PARTS)), dma((n, PARTS)), dma((n,)), dma((n,)),
            dma((n,)), dma((n,)), dma((n,)), dma((ns,)), dma((ns,)),
        ],
        compiler_params=pltpu.CompilerParams(
            collective_id=0, has_side_effects=True, vmem_limit_bytes=44 * 1024 * 1024
        ),
    )(
        *(
            pltpu.with_memory_space_constraint(value, pltpu.HBM)
            for value in (
                src_vel,
                angle.reshape(sb, BLK),
                src_block.reshape(n, cap),
                tgt_block.reshape(n, cap),
                send_count.reshape(n),
                intersection.reshape(n, cap, BLK, BLK),
                eo,
            )
        )
    )
    return remapped, pcs


def solution(mesh):
    return jax.shard_map(
        functools.partial(per_device, mesh.shape["tgt"], mesh.shape["src"]),
        mesh=mesh,
        in_specs=(
            P(None, None, ("src", "tgt")),
            P(("src", "tgt")),
            P("src", "tgt", None, None),
            P("src", "tgt", None, None),
            P("src", "tgt", None),
            P("src", "tgt", None, None, None, None),
            P(None, None, ("src", "tgt")),
        ),
        out_specs=(P(None, None, ("src", "tgt")), P(None, "tgt")),
        check_vma=False,
    )
```
